256 devices in a mesh: rows: 32 (over y, z), feat: 8 (over x, core).
Axes of the slice: x: 4, y: 4, z: 8, core: 2. Of those that a mesh axis runs over, the one named last changes fastest.
Arguments:
- targets: bfloat16 [131072, 1024], P('rows', 'feat'), may hold values from -6 to 6
- omega: bfloat16 [1024, 256], P('feat'), may hold values from -0.1875 to 0.1875
- phase: float32 [256], replicated, may hold values from -3.140625 to 3.140625
- codes: int32 [131072, 128], P('rows', 'feat'), may hold values from 0 to 31, as said below
- node: int32 [131072], P('rows'), may hold values from 0 to 7, as said below
- boot_counts: int32 [131072], P('rows'), may hold values from 0 to 3
Outputs:
- gains: float32 [1024, 31], P(('feat', 'rows'))
- best: float32 [8], replicated
The draws below stay inside these ranges and needn't reach their ends.
Inputs may be any that keep to these rules, and one draw needn't show every extreme that they name: `codes`: each feature has a lowest and a highest used bin; some features use bin 0 and some bin 32 - 1. Among the rows of each device every node holds a row with a nonzero bootstrap count.
All inputs are finite; a program needn't handle non-finite values.
Results may differ from the reference program's by a relative error of at most 0.00051.
Values may be sent and summed in bfloat16 or wider, within the bound.
A program may use at most 64 MiB of HBM per device.

```python
import math
import jax
import jax.numpy as jnp
from jax import lax

F = 128
E = 1024
R = 256
BINS = 32
NODES = 8
ROWS_DEV = 4096
ROWS = 131072


def draw_codes(key, part):
    first = jax.random.fold_in(key, 11)
    second = jax.random.fold_in(key, 12)
    third = jax.random.fold_in(key, 13)
    raw = jax.random.randint(first, (ROWS, F), 0, BINS)
    feature_id = jnp.arange(F)
    lowest = jax.random.randint(second, (F,), 0, 6) * (feature_id % 4 != 0).astype(jnp.int32)
    highest = BINS - 1 - jax.random.randint(third, (F,), 0, 6) * (feature_id % 4 != 1).astype(jnp.int32)
    return jnp.clip(raw, lowest[None, :], highest[None, :]).astype(jnp.int32)


def draw_node(key, part):
    raw = jax.random.randint(jax.random.fold_in(key, 21), (ROWS,), 0, NODES)
    position = jnp.arange(ROWS) % ROWS_DEV
    return jnp.where(position < NODES, position, raw).astype(jnp.int32)


def draw_boot_counts(key, part):
    raw = jax.random.randint(jax.random.fold_in(key, 31), (ROWS,), 0, 4)
    position = jnp.arange(ROWS) % ROWS_DEV
    return jnp.where(position < NODES, jnp.maximum(raw, 1), raw).astype(jnp.int32)


def levels(stream_key, extent, pieces, low, largest):
    factor_of = 1.0
    for dim, parts in pieces:
        draws = jax.random.uniform(jax.random.fold_in(jax.random.fold_in(stream_key, 6), dim), (parts,), jnp.float32, low / len(pieces), largest / len(pieces))
        factor_of = factor_of * jnp.repeat(jnp.exp(draws), extent[dim] // parts).reshape((-1,) + (1,) * (len(extent) - 1 - dim))
    return factor_of


def gaussian(stream_key, extent, width, most, cuts=(), kind=jnp.bfloat16):
    array = jax.random.normal(stream_key, extent, jnp.float32) * width
    if len(cuts) > 0:
        array = levels(stream_key, extent, cuts, -0.22, 0.18) * array
    return jnp.clip(array, min=-most, max=most).astype(kind)


def setup_inputs(seed: int = 0) -> dict:
    key_of = jax.random.split(jax.random.key(seed), 7)
    targets = gaussian(key_of[0], (ROWS, E), 1.0, 6.0, ((0, 32), (1, 8)))
    omega = gaussian(key_of[1], (E, R), E ** -0.5, 0.1875, ((0, 8),))
    phase = jnp.clip(jax.random.uniform(key_of[2], (R,), jnp.float32, -3.140625, 3.140625), -3.140625, 3.140625)
    codes = draw_codes(jax.random.fold_in(key_of[6], 71), 0)
    node = draw_node(jax.random.fold_in(key_of[6], 71), 0)
    boot_counts = draw_boot_counts(jax.random.fold_in(key_of[6], 71), 0)
    return dict(targets=targets, omega=omega, phase=phase, codes=codes, node=node, boot_counts=boot_counts)


def split_gains(sums, tallies):
    left = jnp.cumsum(sums, axis=1)[:, :-1, :]
    whole = lax.optimization_barrier(jnp.sum(sums, axis=1))
    left_count = jnp.cumsum(tallies, axis=1)[:, :-1]
    total = lax.optimization_barrier(jnp.sum(tallies, axis=1))
    right_count = total[:, None] - left_count
    right = whole[:, None, :] - left
    differ = left / jnp.maximum(left_count, 1.0)[:, :, None] - right / jnp.maximum(right_count, 1.0)[:, :, None]
    factor = left_count * right_count / total[:, None]
    return factor * lax.optimization_barrier(jnp.sum(differ * differ, axis=2))

def reference(targets, omega, phase, codes, node, boot_counts):
    projected = jnp.dot(targets.astype(jnp.float32), omega.astype(jnp.float32), precision=lax.Precision.HIGHEST)
    fourier = (math.sqrt(2.0 / R) * jnp.cos(projected + phase[None, :])).astype(jnp.bfloat16)
    weights = boot_counts.astype(jnp.float32)
    weighted = weights[:, None] * fourier.astype(jnp.float32)
    slot_base = node * BINS

    def per_feature(column):
        index = slot_base + column
        sums = jax.ops.segment_sum(weighted, index, num_segments=NODES * BINS)
        tallies = jax.ops.segment_sum(weights, index, num_segments=NODES * BINS)
        return (sums, tallies)
    histogram, tallies = lax.map(per_feature, codes.T)
    histogram = histogram.reshape(F * NODES, BINS, R)
    tallies = tallies.reshape(F * NODES, BINS)
    gains = split_gains(histogram, tallies)
    best = lax.optimization_barrier(jnp.max(gains.reshape(F, NODES, BINS - 1), axis=(0, 2)))
    return (gains, best)
```

```python
import functools
import math

import jax
import jax.numpy as jnp
from jax import lax
from jax.experimental import pallas as pl
from jax.experimental.pallas import tpu as pltpu
from jax.sharding import PartitionSpec as P

MESH = pl.DeviceIdType.MESH
HIGH = lax.Precision.HIGHEST
F32 = jnp.float32
BF16 = jnp.bfloat16

R = 256
BINS = 32
NODES = 8
X = 4
Y = 4
Z = 8
FEAT = 2 * X
FD = 16
RD = 4096
CH = RD // FEAT
CO = R // Z
EXT = RD + CH
DELTA = (0, 1, -1, 2, -2, 3, -3, 4)

NT = (((1,), (1,)), ((), ()))
TN = (((0,), (0,)), ((), ()))

TWO_PI = 2.0 * math.pi
C1 = 6.28125
C2 = TWO_PI - C1
COS = [(-1.0) ** i / math.factorial(2 * i) for i in range(9)]


def cosine(v):
    turns = jnp.floor(v * (1.0 / TWO_PI) + 0.5)
    r = (v - turns * C1) - turns * C2
    x = r * r
    acc = jnp.full_like(x, COS[8])
    for c in COS[7::-1]:
        acc = acc * x + c
    return acc


def iota(shape, dim):
    return lax.broadcasted_iota(jnp.int32, shape, dim)


def kernel(tg, om, ph, codes, node, boot, out, best,
           t_buf, om_buf, omt, phc, cb, x32, oh, rn, ft, proj, fb, acc, sb, rb,
           ts, ta, tsum, tb, gb, bm, by, bf, ssem, rsem, lsem):
    rows = lax.axis_index("rows")
    me = lax.axis_index("feat")
    y, z = rows // Z, rows % Z
    x, core = me // 2, me % 2

    def at_z(d):
        return {"rows": y * Z + (z + d + Z) % Z}

    def at_y(d):
        return {"rows": ((y + d) % Y) * Z + z}

    def at_feat(d):
        return {"feat": (me + d) % FEAT}

    def at_x(d):
        return {"feat": ((x + d) % X) * 2 + core}

    sibling = {"feat": x * 2 + 1 - core}

    barrier = pltpu.get_barrier_semaphore()
    for d in range(1, FEAT):
        pl.semaphore_signal(barrier, inc=1, device_id=at_feat(d), device_id_type=MESH)
    for d in range(1, Z):
        pl.semaphore_signal(barrier, inc=1, device_id=at_z(d), device_id_type=MESH)
    for d in range(1, Y):
        pl.semaphore_signal(barrier, inc=1, device_id=at_y(d), device_id_type=MESH)

    cb[z, :, 0:RD] = codes[...].astype(F32).astype(BF16)
    for q in range(4):
        nq = node[pl.ds(q, FEAT, stride=4), :].astype(F32)
        wq = boot[pl.ds(q, FEAT, stride=4), :].astype(F32)
        both = jnp.concatenate([nq, wq], axis=0)
        cb[z, :, RD + 128 * q:RD + 128 * (q + 1)] = both.astype(BF16)

    pl.semaphore_wait(barrier, FEAT - 1 + Z - 1 + Y - 1)

    sends = []

    def send(src, dst, dev):
        i = len(sends)
        copy = pltpu.make_async_remote_copy(
            src_ref=src, dst_ref=dst, send_sem=ssem.at[i], recv_sem=rsem.at[i],
            device_id=dev, device_id_type=MESH)
        copy.start()
        sends.append(copy)
        return copy

    def row_block(i):
        return pl.ds(pl.multiple_of(i * CH, CH), CH)

    mine = pl.ds(pl.multiple_of(me * 128, 128), 128)
    om_in = [send(om, om_buf.at[mine, :], dev)
             for dev in (at_x(2), at_x(1), at_x(3), sibling)]
    c_r = send(cb.at[z], cb.at[z], at_z(1))
    c_l = send(cb.at[z], cb.at[z], at_z(-1))
    t_in = []
    for d in (4, 5, 3, 2, 6, 1, 7):
        peer = (me + d) % FEAT
        t_in.append(send(tg.at[row_block(peer), :], t_buf.at[:, mine], at_feat(d)))
    own_t = pltpu.make_async_copy(tg.at[row_block(me), :], t_buf.at[:, mine], lsem.at[0])
    own_t.start()
    own_o = pltpu.make_async_copy(om, om_buf.at[mine, :], lsem.at[1])
    own_o.start()

    def one_hot(zs, start, which):
        c = cb[zs, :, pl.ds(start, CH)]
        w = jnp.broadcast_to(x32[pl.ds(which + FEAT, 1), :], (FD, CH)).astype(BF16)
        zero = jnp.zeros_like(w)
        return [jnp.where(c == jnp.asarray(b, BF16), w, zero) for b in range(BINS)]

    x32[...] = cb[z, :, RD:EXT].astype(F32)
    acc[...] = jnp.zeros_like(acc)
    nt = jnp.zeros((FD, BINS * FD), F32)
    acc_t = proj.at[0:FD, :]
    acc_t[...] = nt

    @pl.loop(0, FEAT)
    def _(jj):
        for b, part in enumerate(one_hot(z, pl.multiple_of(jj * CH, CH), jj)):
            oh[0, b * FD:(b + 1) * FD, :] = part
        nd = jnp.broadcast_to(x32[pl.ds(jj, 1), :], (FD, CH)).astype(BF16)
        ids = iota((FD, CH), 0).astype(F32).astype(BF16)
        noh = jnp.where(nd == ids, jnp.ones_like(nd), jnp.zeros_like(nd))
        acc_t[...] += lax.dot_general(noh, oh[0], NT, preferred_element_type=F32)

    tl = acc_t[0:NODES, :]
    r_id, l_id = iota((BINS * FD, 128), 0), iota((BINS * FD, 128), 1)
    for yy in range(Y):
        sel = (r_id // FD == l_id // 4) & (r_id % FD == 4 * yy + l_id % 4)
        ts[yy] = jnp.dot(tl, sel.astype(F32), precision=HIGH, preferred_element_type=F32)
    ty_in = [send(ts.at[(y + d) % Y], ta.at[d], at_y(d)) for d in (2, 1, 3)]

    phc[...] = jnp.broadcast_to(ph[...], (128, R)).T

    c_r.wait_recv()
    c_l.wait_recv()
    c_r = send(cb.at[(z + Z - 1) % Z], cb.at[(z + Z - 1) % Z], at_z(1))
    c_l = send(cb.at[(z + 1) % Z], cb.at[(z + 1) % Z], at_z(-1))

    for c in ty_in:
        c.wait_recv()
    tsum[...] = ts[y] + ta[1] + ta[2] + ta[3]
    tz_in = [send(tsum, tb.at[d], at_z(d)) for d in range(1, Z)]

    c_r.wait_recv()
    c_l.wait_recv()
    c_r = send(cb.at[(z + Z - 2) % Z], cb.at[(z + Z - 2) % Z], at_z(1))
    c_l = send(cb.at[(z + 2) % Z], cb.at[(z + 2) % Z], at_z(-1))

    for c in om_in:
        c.wait_recv()
    om_fwd = []
    for d in (1, 2, 3):
        src = pl.ds(pl.multiple_of((((x + d) % X) * 2 + core) * 128, 128), 128)
        om_fwd.append(send(om_buf.at[src, :], om_buf.at[src, :], sibling))

    for c in tz_in:
        c.wait_recv()
    total = tsum[...]
    for d in range(1, Z):
        total = total + tb[d]

    c_r.wait_recv()
    c_l.wait_recv()
    lo, hi = pl.ds(0, EXT // 2), pl.ds(EXT // 2, EXT // 2)
    c_r = send(cb.at[(z + Z - 3) % Z, :, lo], cb.at[(z + Z - 3) % Z, :, lo], at_z(1))
    c_l = send(cb.at[(z + 3) % Z, :, hi], cb.at[(z + 3) % Z, :, hi], at_z(-1))

    own_o.wait()
    for c in om_fwd:
        c.wait_recv()
    omt[...] = om_buf[...].astype(F32).T.astype(BF16)

    own_t.wait()
    for c in t_in:
        c.wait_recv()
    proj[...] = lax.dot_general(omt[...], t_buf[...], NT, preferred_element_type=F32)
    scaling = math.sqrt(2.0 / R)

    @pl.loop(0, R // 32)
    def _(i):
        at = pl.ds(pl.multiple_of(i * 32, 32), 32)
        column = phc[at, :]
        for q in range(CH // 128):
            lane = slice(128 * q, 128 * (q + 1))
            ft[i, :, lane] = (scaling * cosine(proj[at, lane] + column)).astype(BF16)

    own_f = pltpu.make_async_copy(ft.at[z], fb.at[me, z], lsem.at[2])
    own_f.start()
    z_in = [None]
    for k in range(1, Z):
        z_in.append(send(ft.at[(z - DELTA[k] + Z) % Z], fb.at[me, z], at_z(-DELTA[k])))
    c_r.wait_recv()
    c_l.wait_recv()
    own_f.wait()

    def hist(zs):
        x32[...] = cb[zs, :, RD:EXT].astype(F32)

        @pl.loop(0, FEAT // 2)
        def _(i):
            for h in range(2):
                jj = 2 * i + h
                for b, part in enumerate(one_hot(zs, pl.multiple_of(jj * CH, CH), jj)):
                    oh[h, b * FD:(b + 1) * FD, :] = part
                nd = jnp.broadcast_to(x32[pl.ds(jj, 1), :], (FD, CH)).astype(BF16)
                f = fb[jj, zs]
                zero = jnp.zeros((FD, CH), BF16)
                for n in range(NODES):
                    mask = nd == jnp.asarray(n, BF16)
                    for g in range(CO // FD):
                        rn[h, n * CO + g * FD:n * CO + (g + 1) * FD, :] = jnp.where(
                            mask, f[g * FD:(g + 1) * FD], zero)
            acc[...] += (lax.dot_general(oh[0], rn[0], NT, preferred_element_type=F32)
                         + lax.dot_general(oh[1], rn[1], NT, preferred_element_type=F32))

    a_in, b_in, c_in = {}, {}, {}
    own_to = lambda d: ((x + d) % X) * 2 + core
    for it in range(Z + 3):
        if it < Z:
            k = it
            zs = (z + DELTA[k] + Z) % Z
            if k > 0:
                z_in[k].wait_recv()
            blk = fb.at[me, zs]
            a_in[k] = [send(blk, blk, at_x(1)), send(blk, blk, at_x(-1 + X)),
                       send(blk, blk, sibling)]
        if 0 <= it - 1 < Z:
            k = it - 1
            zs = (z + DELTA[k] + Z) % Z
            from_left, from_right, from_sib = a_in[k]
            from_left.wait_recv()
            from_right.wait_recv()
            lb, rbk = fb.at[own_to(3), zs], fb.at[own_to(1), zs]
            if k % 2 == 0:
                opp = send(lb, lb, at_x(1))
            else:
                opp = send(rbk, rbk, at_x(3))
            b_in[k] = [opp, send(lb, lb, sibling), send(rbk, rbk, sibling)]
        if 0 <= it - 2 < Z:
            k = it - 2
            zs = (z + DELTA[k] + Z) % Z
            b_in[k][0].wait_recv()
            ob = fb.at[own_to(2), zs]
            c_in[k] = send(ob, ob, sibling)
        if 0 <= it - 3 < Z:
            k = it - 3
            zs = (z + DELTA[k] + Z) % Z
            a_in[k][2].wait_recv()
            b_in[k][1].wait_recv()
            b_in[k][2].wait_recv()
            c_in[k].wait_recv()
            hist(zs)

    for yy in range(Y):
        half, sub = yy // 2, yy % 2
        for bp in range(BINS // 2):
            even = acc[(2 * bp) * FD + 8 * half:(2 * bp) * FD + 8 * half + 8, :]
            odd = acc[(2 * bp + 1) * FD + 8 * half:(2 * bp + 1) * FD + 8 * half + 8, :]
            low = iota((8, R), 0) < 4
            if sub == 0:
                sb[yy, 8 * bp:8 * bp + 8, :] = jnp.where(low, even, pltpu.roll(odd, 4, 0))
            else:
                sb[yy, 8 * bp:8 * bp + 8, :] = jnp.where(low, pltpu.roll(even, 4, 0), odd)
    y_in = [send(sb.at[(y + d) % Y], rb.at[d], at_y(d)) for d in (2, 1, 3)]

    r128, l128 = iota((128, 128), 0), iota((128, 128), 1)
    same = r128 % 4 == l128 % 4
    upto = (same & (l128 // 4 <= r128 // 4)).astype(F32)
    every = same.astype(F32)
    left_n = lax.dot_general(total, upto, NT, precision=HIGH, preferred_element_type=F32)
    all_n = lax.dot_general(total, every, NT, precision=HIGH, preferred_element_type=F32)
    right_n = all_n - left_n
    factor = left_n * right_n / all_n
    expand = (iota((NODES, R), 1) // CO == iota((NODES, R), 0)).astype(F32)
    left_w = lax.dot_general(1.0 / jnp.maximum(left_n, 1.0), expand, TN,
                             precision=HIGH, preferred_element_type=F32)
    right_w = lax.dot_general(1.0 / jnp.maximum(right_n, 1.0), expand, TN,
                              precision=HIGH, preferred_element_type=F32)

    for c in y_in:
        c.wait_recv()
    summed = sb[y] + rb[1] + rb[2] + rb[3]
    left = jnp.dot(upto, summed, precision=HIGH, preferred_element_type=F32)
    whole = jnp.dot(every, summed, precision=HIGH, preferred_element_type=F32)
    differ = left * left_w - (whole - left) * right_w
    gb[z] = lax.dot_general(expand, differ * differ, NT, precision=HIGH,
                            preferred_element_type=F32)
    g_in = [send(gb.at[z], gb.at[z], at_z(d)) for d in (4, 3, 5, 2, 6, 1, 7)]
    for c in g_in:
        c.wait_recv()
    norm = gb[0]
    for d in range(1, Z):
        norm = norm + gb[d]
    gains = factor * norm

    top = jnp.max(jnp.where(iota((NODES, 128), 1) < 4 * (BINS - 1), gains, -jnp.inf),
                  axis=1, keepdims=True)
    bm[...] = jnp.broadcast_to(top, (NODES, 128))
    by_in = [send(bm, by.at[d], at_y(d)) for d in (2, 1, 3)]
    pick = (r128 == 4 * l128 + z // 2).astype(F32)
    picked = jnp.dot(gains, pick, precision=HIGH, preferred_element_type=F32)
    out[...] = jnp.where(z % 2 == 0, picked[0:4], picked[4:8])[:, 0:BINS - 1]
    for c in by_in:
        c.wait_recv()
    bf[0] = jnp.maximum(jnp.maximum(bm[...], by[1]), jnp.maximum(by[2], by[3]))
    bf_in = [send(bf.at[0], bf.at[d], at_feat(d)) for d in (4, 5, 3, 2, 6, 1, 7)]
    for c in bf_in:
        c.wait_recv()
    top = bf[0]
    for d in range(1, FEAT):
        top = jnp.maximum(top, bf[d])
    best[...] = top
    for c in sends:
        c.wait_send()


N_SENDS = 160


def body(targets, omega, phase, codes, node, boot_counts):
    vmem = pl.BlockSpec(memory_space=pltpu.VMEM)
    gains, best = pl.pallas_call(
        kernel,
        out_shape=(jax.ShapeDtypeStruct((4, BINS - 1), F32),
                   jax.ShapeDtypeStruct((NODES, 128), F32)),
        in_specs=[vmem] * 6,
        out_specs=(vmem, vmem),
        scratch_shapes=[
            pltpu.VMEM((CH, 1024), BF16),
            pltpu.VMEM((1024, R), BF16),
            pltpu.VMEM((R, 1024), BF16),
            pltpu.VMEM((R, 128), F32),
            pltpu.VMEM((Z, FD, EXT), BF16),
            pltpu.VMEM((2 * FEAT, CH), F32),
            pltpu.VMEM((2, BINS * FD, CH), BF16),
            pltpu.VMEM((2, NODES * CO, CH), BF16),
            pltpu.VMEM((Z, CO, CH), BF16),
            pltpu.VMEM((R, CH), F32),
            pltpu.VMEM((FEAT, Z, CO, CH), BF16),
            pltpu.VMEM((BINS * FD, R), F32),
            pltpu.VMEM((Y, 128, R), F32),
            pltpu.VMEM((Y, 128, R), F32),
            pltpu.VMEM((Y, NODES, 128), F32),
            pltpu.VMEM((Y, NODES, 128), F32),
            pltpu.VMEM((NODES, 128), F32),
            pltpu.VMEM((Z, NODES, 128), F32),
            pltpu.VMEM((Z, NODES, 128), F32),
            pltpu.VMEM((NODES, 128), F32),
            pltpu.VMEM((Y, NODES, 128), F32),
            pltpu.VMEM((FEAT, NODES, 128), F32),
            pltpu.SemaphoreType.DMA((N_SENDS,)),
            pltpu.SemaphoreType.DMA((N_SENDS,)),
            pltpu.SemaphoreType.DMA((3,)),
        ],
        compiler_params=pltpu.CompilerParams(
            collective_id=0, has_side_effects=True, vmem_limit_bytes=40 * 2 ** 20),
        name="forest_level",
    )(targets, omega, phase.reshape(1, R), codes.T,
      node.reshape(RD // 128, 128), boot_counts.reshape(RD // 128, 128))
    return gains, best[:, 0]


def solution(mesh):
    in_specs = (P("rows", "feat"), P("feat", None), P(), P("rows", "feat"), P("rows"), P("rows"))
    out_specs = (P(("feat", "rows"), None), P())
    return jax.shard_map(body, mesh=mesh, in_specs=in_specs, out_specs=out_specs, check_vma=False)
```

```python
import functools
import math

import jax
import jax.numpy as jnp
from jax import lax
from jax.experimental import pallas as pl
from jax.experimental.pallas import tpu as pltpu
from jax.sharding import PartitionSpec as P

MESH = pl.DeviceIdType.MESH
HIGH = lax.Precision.HIGHEST
F32 = jnp.float32
BF16 = jnp.bfloat16

R = 256
BINS = 32
NODES = 8
X = 4
Y = 4
Z = 8
FEAT = 2 * X
FD = 16
RD = 4096
CH = RD // FEAT
CO = R // Z
EXT = RD + CH
DELTA = (0, 1, -1, 2, -2, 3, -3, 4)

NT = (((1,), (1,)), ((), ()))
TN = (((0,), (0,)), ((), ()))

TWO_PI = 2.0 * math.pi
C1 = 6.28125
C2 = TWO_PI - C1
COS = [(-1.0) ** i / math.factorial(2 * i) for i in range(9)]


def cosine(v):
    turns = jnp.floor(v * (1.0 / TWO_PI) + 0.5)
    r = (v - turns * C1) - turns * C2
    x = r * r
    acc = jnp.full_like(x, COS[8])
    for c in COS[7::-1]:
        acc = acc * x + c
    return acc


def iota(shape, dim):
    return lax.broadcasted_iota(jnp.int32, shape, dim)


def kernel(tg, om, ph_h, codes_h, node_h, boot_h, out, best,
           ph, codes, node, boot, t_buf, om_buf, omt, phc, cb, x32, oh, rn, ft, proj, fb, acc, sb, rb,
           ts, ta, tsum, tb, gb, bm, by, ssem, rsem, lsem):
    rows = lax.axis_index("rows")
    me = lax.axis_index("feat")
    y, z = rows // Z, rows % Z
    x, core = me // 2, me % 2

    def at_z(d):
        return {"rows": y * Z + (z + d + Z) % Z}

    def at_y(d):
        return {"rows": ((y + d) % Y) * Z + z}

    def at_feat(d):
        return {"feat": (me + d) % FEAT}

    def at_x(d):
        return {"feat": ((x + d) % X) * 2 + core}

    def at_plane(dy, d):
        return {"rows": ((y + dy) % Y) * Z + z, "feat": (me + d) % FEAT}

    sibling = {"feat": x * 2 + 1 - core}

    loads = [pltpu.make_async_copy(a, b, lsem.at[3 + i]) for i, (a, b) in enumerate(
        ((codes_h, codes), (node_h, node), (boot_h, boot), (ph_h, ph)))]
    for c in loads:
        c.start()
    barrier = pltpu.get_barrier_semaphore()
    for d in range(1, FEAT):
        pl.semaphore_signal(barrier, inc=1, device_id=at_feat(d), device_id_type=MESH)
    for d in range(1, Z):
        pl.semaphore_signal(barrier, inc=1, device_id=at_z(d), device_id_type=MESH)
    for dy in range(1, Y):
        for d in range(FEAT):
            pl.semaphore_signal(barrier, inc=1, device_id=at_plane(dy, d), device_id_type=MESH)

    for c in loads:
        c.wait()
    cb[z, :, 0:RD] = codes[...].astype(F32).astype(BF16)
    for q in range(4):
        nq = node[pl.ds(q, FEAT, stride=4), :].astype(F32)
        wq = boot[pl.ds(q, FEAT, stride=4), :].astype(F32)
        both = jnp.concatenate([nq, wq], axis=0)
        cb[z, :, RD + 128 * q:RD + 128 * (q + 1)] = both.astype(BF16)

    pl.semaphore_wait(barrier, Z - 1 + Y * FEAT - 1)

    sends = []

    def send(what, src, dst, dev):
        i = len(sends)
        copy = pltpu.make_async_remote_copy(
            src_ref=src, dst_ref=dst, send_sem=ssem.at[i], recv_sem=rsem.at[i],
            device_id=dev, device_id_type=MESH)
        copy.start()
        sends.append(copy)
        return copy

    def row_block(i):
        return pl.ds(pl.multiple_of(i * CH, CH), CH)

    mine = pl.ds(pl.multiple_of(me * 128, 128), 128)

    def quarter(j):
        return pl.ds(pl.multiple_of(j * 128 + y * 32, 32), 32)

    own_q = om.at[pl.ds(pl.multiple_of(y * 32, 32), 32), :]
    om_in = [send("om", own_q, om_buf.at[quarter(me), :], at_x(d)) for d in (2, 1, 3)]
    om_sib = send("om", om, om_buf.at[mine, :], sibling)
    c_r = send("codes", cb.at[z], cb.at[z], at_z(1))
    c_l = send("codes", cb.at[z], cb.at[z], at_z(-1))
    t_in = []
    for d in (4, 5, 3, 2, 6, 1, 7):
        peer = (me + d) % FEAT
        t_in.append(send("t", tg.at[row_block(peer), :], t_buf.at[:, mine], at_feat(d)))
    own_t = pltpu.make_async_copy(tg.at[row_block(me), :], t_buf.at[:, mine], lsem.at[0])
    own_t.start()
    own_o = pltpu.make_async_copy(om, om_buf.at[mine, :], lsem.at[1])
    own_o.start()

    def one_hot(zs, start, which):
        c = cb[zs, :, pl.ds(start, CH)]
        w = jnp.broadcast_to(x32[pl.ds(which + FEAT, 1), :], (FD, CH)).astype(BF16)
        zero = jnp.zeros_like(w)
        return [jnp.where(c == jnp.asarray(b, BF16), w, zero) for b in range(BINS)]

    x32[...] = cb[z, :, RD:EXT].astype(F32)
    acc[...] = jnp.zeros_like(acc)
    nt = jnp.zeros((FD, BINS * FD), F32)
    acc_t = proj.at[0:FD, :]
    acc_t[...] = nt

    @pl.loop(0, FEAT)
    def _(jj):
        for b, part in enumerate(one_hot(z, pl.multiple_of(jj * CH, CH), jj)):
            oh[0, b * FD:(b + 1) * FD, :] = part
        nd = jnp.broadcast_to(x32[pl.ds(jj, 1), :], (FD, CH)).astype(BF16)
        ids = iota((FD, CH), 0).astype(F32).astype(BF16)
        noh = jnp.where(nd == ids, jnp.ones_like(nd), jnp.zeros_like(nd))
        acc_t[...] += lax.dot_general(noh, oh[0], NT, preferred_element_type=F32)

    tl = acc_t[0:NODES, :]
    r_id, l_id = iota((BINS * FD, 128), 0), iota((BINS * FD, 128), 1)
    for yy in range(Y):
        sel = (r_id // FD == l_id // 4) & (r_id % FD == 4 * yy + l_id % 4)
        ts[yy] = jnp.dot(tl, sel.astype(F32), precision=HIGH, preferred_element_type=F32)
    ty_in = [send("ty", ts.at[(y + d) % Y], ta.at[d], at_y(d)) for d in (2, 1, 3)]

    phc[...] = jnp.broadcast_to(ph[...], (128, R)).T

    c_r.wait_recv()
    c_l.wait_recv()
    c_r = send("codes", cb.at[(z + Z - 1) % Z], cb.at[(z + Z - 1) % Z], at_z(1))
    c_l = send("codes", cb.at[(z + 1) % Z], cb.at[(z + 1) % Z], at_z(-1))

    om_y = []
    for i, d in enumerate((2, 1, 3)):
        om_in[i].wait_recv()
    for d in (2, 1, 3):
        blk = om_buf.at[quarter(((x + d) % X) * 2 + core), :]
        for dy in (2, 1, 3):
            om_y.append(send("om", blk, blk, at_y(dy)))

    for c in ty_in:
        c.wait_recv()
    tsum[...] = ts[y] + ta[1] + ta[2] + ta[3]
    tz_in = [send("tz", tsum, tb.at[d], at_z(d)) for d in range(1, Z)]

    for c in om_y:
        c.wait_recv()
    om_fwd = [om_sib]
    for d in (1, 2, 3):
        src = pl.ds(pl.multiple_of((((x + d) % X) * 2 + core) * 128, 128), 128)
        om_fwd.append(send("omf", om_buf.at[src, :], om_buf.at[src, :], sibling))

    c_r.wait_recv()
    c_l.wait_recv()
    c_r = send("codes", cb.at[(z + Z - 2) % Z], cb.at[(z + Z - 2) % Z], at_z(1))
    c_l = send("codes", cb.at[(z + 2) % Z], cb.at[(z + 2) % Z], at_z(-1))

    own_o.wait()
    for c in om_fwd:
        c.wait_recv()
    omt[...] = om_buf[...].astype(F32).T.astype(BF16)

    own_t.wait()
    for c in t_in:
        c.wait_recv()
    proj[...] = lax.dot_general(omt[...], t_buf[...], NT, preferred_element_type=F32)
    scaling = math.sqrt(2.0 / R)

    @pl.loop(0, R // 32)
    def _(i):
        at = pl.ds(pl.multiple_of(i * 32, 32), 32)
        column = phc[at, :]
        for q in range(CH // 128):
            lane = slice(128 * q, 128 * (q + 1))
            ft[i, :, lane] = (scaling * cosine(proj[at, lane] + column)).astype(BF16)

    own_f = pltpu.make_async_copy(ft.at[z], fb.at[me, z], lsem.at[2])
    own_f.start()
    z_in = [None]
    for k in range(1, Z):
        z_in.append(send("fz", ft.at[(z - DELTA[k] + Z) % Z], fb.at[me, z], at_z(-DELTA[k])))
    own_f.wait()

    def hist(zs):
        x32[...] = cb[zs, :, RD:EXT].astype(F32)

        @pl.loop(0, FEAT // 2)
        def _(i):
            for h in range(2):
                jj = 2 * i + h
                for b, part in enumerate(one_hot(zs, pl.multiple_of(jj * CH, CH), jj)):
                    oh[h, b * FD:(b + 1) * FD, :] = part
                nd = jnp.broadcast_to(x32[pl.ds(jj, 1), :], (FD, CH)).astype(BF16)
                f = fb[jj, zs]
                zero = jnp.zeros((FD, CH), BF16)
                for n in range(NODES):
                    mask = nd == jnp.asarray(n, BF16)
                    for g in range(CO // FD):
                        rn[h, n * CO + g * FD:n * CO + (g + 1) * FD, :] = jnp.where(
                            mask, f[g * FD:(g + 1) * FD], zero)
            acc[...] += (lax.dot_general(oh[0], rn[0], NT, preferred_element_type=F32)
                         + lax.dot_general(oh[1], rn[1], NT, preferred_element_type=F32))

    a_in, b_in, c_in = {}, {}, {}

    def from_x(d):
        return ((x + d) % X) * 2 + core

    def stage_a(k, zs):
        if k > 0:
            z_in[k].wait_recv()
        blk = fb.at[me, zs]
        a_in[k] = [send("fx", blk, blk, at_x(1)), send("fx", blk, blk, at_x(3)),
                   send("fs", blk, blk, sibling)]

    def stage_b(k, zs):
        a_in[k][0].wait_recv()
        a_in[k][1].wait_recv()
        left, right = fb.at[from_x(3), zs], fb.at[from_x(1), zs]
        opp = (send("fo", left, left, at_x(1)) if k % 2 == 0
               else send("fo", right, right, at_x(3)))
        b_in[k] = [opp, send("fs", left, left, sibling), send("fs", right, right, sibling)]

    def stage_c(k, zs):
        b_in[k][0].wait_recv()
        opp = fb.at[from_x(2), zs]
        c_in[k] = send("fs", opp, opp, sibling)

    def stage_d(k, zs):
        a_in[k][2].wait_recv()
        b_in[k][1].wait_recv()
        b_in[k][2].wait_recv()
        c_in[k].wait_recv()
        hist(zs)

    stages = {"A": stage_a, "B": stage_b, "C": stage_c, "D": stage_d}

    def run(order):
        for item in order.split():
            k = int(item[1])
            stages[item[0]](k, (z + DELTA[k] + Z) % Z)

    run("A0 A1 A2")
    c_r.wait_recv()
    c_l.wait_recv()
    lo, hi = pl.ds(0, EXT // 2), pl.ds(EXT // 2, EXT // 2)
    c_r = send("codes", cb.at[(z + Z - 3) % Z, :, lo], cb.at[(z + Z - 3) % Z, :, lo], at_z(1))
    c_l = send("codes", cb.at[(z + 3) % Z, :, hi], cb.at[(z + 3) % Z, :, hi], at_z(-1))
    run("B0 A3 A4 B1 B2 C0 A5 A6 B3 B4 C1 C2 D0 A7 B5 B6 C3 C4 D1 D2 B7 C5 C6 D3 D4 C7 D5 D6")
    c_r.wait_recv()
    c_l.wait_recv()
    run("D7")
    for yy in range(Y):
        half, sub = yy // 2, yy % 2
        for bp in range(BINS // 2):
            even = acc[(2 * bp) * FD + 8 * half:(2 * bp) * FD + 8 * half + 8, :]
            odd = acc[(2 * bp + 1) * FD + 8 * half:(2 * bp + 1) * FD + 8 * half + 8, :]
            low = iota((8, R), 0) < 4
            if sub == 0:
                sb[yy, 8 * bp:8 * bp + 8, :] = jnp.where(low, even, pltpu.roll(odd, 4, 0))
            else:
                sb[yy, 8 * bp:8 * bp + 8, :] = jnp.where(low, pltpu.roll(even, 4, 0), odd)
    y_in = [send("y", sb.at[(y + d) % Y], rb.at[d], at_y(d)) for d in (2, 1, 3)]

    for c in tz_in:
        c.wait_recv()
    total = tsum[...]
    for d in range(1, Z):
        total = total + tb[d]
    r128, l128 = iota((128, 128), 0), iota((128, 128), 1)
    same = r128 % 4 == l128 % 4
    upto = (same & (l128 // 4 <= r128 // 4)).astype(F32)
    every = same.astype(F32)
    left_n = lax.dot_general(total, upto, NT, precision=HIGH, preferred_element_type=F32)
    all_n = lax.dot_general(total, every, NT, precision=HIGH, preferred_element_type=F32)
    right_n = all_n - left_n
    factor = left_n * right_n / all_n
    expand = (iota((NODES, R), 1) // CO == iota((NODES, R), 0)).astype(F32)
    left_w = lax.dot_general(1.0 / jnp.maximum(left_n, 1.0), expand, TN,
                             precision=HIGH, preferred_element_type=F32)
    right_w = lax.dot_general(1.0 / jnp.maximum(right_n, 1.0), expand, TN,
                              precision=HIGH, preferred_element_type=F32)

    for c in y_in:
        c.wait_recv()
    summed = sb[y] + rb[1] + rb[2] + rb[3]
    left = jnp.dot(upto, summed, precision=HIGH, preferred_element_type=F32)
    whole = jnp.dot(every, summed, precision=HIGH, preferred_element_type=F32)
    differ = left * left_w - (whole - left) * right_w
    gb[z] = lax.dot_general(expand, differ * differ, NT, precision=HIGH,
                            preferred_element_type=F32)
    g_in = [send("g", gb.at[z], gb.at[z], at_z(d)) for d in (4, 3, 5, 2, 6, 1, 7)]
    for c in g_in:
        c.wait_recv()
    norm = gb[0]
    for d in range(1, Z):
        norm = norm + gb[d]
    gains = factor * norm

    top = jnp.max(jnp.where(iota((NODES, 128), 1) < 4 * (BINS - 1), gains, -jnp.inf),
                  axis=1, keepdims=True)
    bm[...] = jnp.broadcast_to(top, (NODES, 128))
    b_in = [send("best", bm, by.at[dy, d], at_plane(dy, d))
            for dy in (2, 1, 3, 0) for d in (4, 5, 3, 2, 6, 1, 7, 0) if dy + d]
    pick = (r128 == 4 * l128 + z // 2).astype(F32)
    picked = jnp.dot(gains, pick, precision=HIGH, preferred_element_type=F32)
    out[...] = jnp.where(z % 2 == 0, picked[0:4], picked[4:8])[:, 0:BINS - 1]
    for c in b_in:
        c.wait_recv()
    top = bm[...]
    for dy in range(Y):
        for d in range(FEAT):
            if dy + d:
                top = jnp.maximum(top, by[dy, d])
    best[...] = top
    for c in sends:
        c.wait_send()


N_SENDS = 160


def body(targets, omega, phase, codes, node, boot_counts):
    vmem = pl.BlockSpec(memory_space=pltpu.VMEM)
    gains, best = pl.pallas_call(
        kernel,
        out_shape=(jax.ShapeDtypeStruct((4, BINS - 1), F32),
                   jax.ShapeDtypeStruct((NODES, 128), F32)),
        in_specs=[pl.BlockSpec(memory_space=pltpu.MemorySpace.HBM)] * 6,
        out_specs=(vmem, vmem),
        scratch_shapes=[
            pltpu.VMEM((1, R), F32),
            pltpu.VMEM((FD, RD), jnp.int32),
            pltpu.VMEM((RD // 128, 128), jnp.int32),
            pltpu.VMEM((RD // 128, 128), jnp.int32),
            pltpu.VMEM((CH, 1024), BF16),
            pltpu.VMEM((1024, R), BF16),
            pltpu.VMEM((R, 1024), BF16),
            pltpu.VMEM((R, 128), F32),
            pltpu.VMEM((Z, FD, EXT), BF16),
            pltpu.VMEM((2 * FEAT, CH), F32),
            pltpu.VMEM((2, BINS * FD, CH), BF16),
            pltpu.VMEM((2, NODES * CO, CH), BF16),
            pltpu.VMEM((Z, CO, CH), BF16),
            pltpu.VMEM((R, CH), F32),
            pltpu.VMEM((FEAT, Z, CO, CH), BF16),
            pltpu.VMEM((BINS * FD, R), F32),
            pltpu.VMEM((Y, 128, R), F32),
            pltpu.VMEM((Y, 128, R), F32),
            pltpu.VMEM((Y, NODES, 128), F32),
            pltpu.VMEM((Y, NODES, 128), F32),
            pltpu.VMEM((NODES, 128), F32),
            pltpu.VMEM((Z, NODES, 128), F32),
            pltpu.VMEM((Z, NODES, 128), F32),
            pltpu.VMEM((NODES, 128), F32),
            pltpu.VMEM((Y, FEAT, NODES, 128), F32),
            pltpu.SemaphoreType.DMA((N_SENDS,)),
            pltpu.SemaphoreType.DMA((N_SENDS,)),
            pltpu.SemaphoreType.DMA((7,)),
        ],
        compiler_params=pltpu.CompilerParams(
            collective_id=0, has_side_effects=True),
        name="forest_level",
    )(targets, omega, phase.reshape(1, R), codes.T,
      node.reshape(RD // 128, 128), boot_counts.reshape(RD // 128, 128))
    return gains, best[:, 0]


def solution(mesh):
    in_specs = (P("rows", "feat"), P("feat", None), P(), P("rows", "feat"), P("rows"), P("rows"))
    out_specs = (P(("feat", "rows"), None), P())
    return jax.shard_map(body, mesh=mesh, in_specs=in_specs, out_specs=out_specs, check_vma=False)
```

```python
import functools
import math

import jax
import jax.numpy as jnp
from jax import lax
from jax.experimental import pallas as pl
from jax.experimental.pallas import tpu as pltpu
from jax.sharding import PartitionSpec as P

MESH = pl.DeviceIdType.MESH
HIGH = lax.Precision.HIGHEST
F32 = jnp.float32
BF16 = jnp.bfloat16

R = 256
BINS = 32
NODES = 8
X = 4
Y = 4
Z = 8
FEAT = 2 * X
FD = 16
RD = 4096
CH = RD // FEAT
CO = R // Z
EXT = RD + CH
DELTA = (0, 1, -1, 2, -2, 3, -3, 4)

NT = (((1,), (1,)), ((), ()))
TN = (((0,), (0,)), ((), ()))

TWO_PI = 2.0 * math.pi
C1 = 6.28125
C2 = TWO_PI - C1
COS = [(-1.0) ** i / math.factorial(2 * i) for i in range(9)]


def cosine(v):
    turns = jnp.floor(v * (1.0 / TWO_PI) + 0.5)
    r = (v - turns * C1) - turns * C2
    x = r * r
    acc = jnp.full_like(x, COS[8])
    for c in COS[7::-1]:
        acc = acc * x + c
    return acc


def iota(shape, dim):
    return lax.broadcasted_iota(jnp.int32, shape, dim)


def kernel(tg, om, ph_h, codes_h, node_h, boot_h, out, best,
           ph, codes, node, boot, t_buf, om_buf, omt, phc, cb, x32, oh, rn, ft, proj, fb, acc, sb, rb,
           ts, ta, tsum, tb, gb, bm, by, ssem, rsem, lsem):
    rows = lax.axis_index("rows")
    me = lax.axis_index("feat")
    y, z = rows // Z, rows % Z
    x, core = me // 2, me % 2

    def at_z(d):
        return {"rows": y * Z + (z + d + Z) % Z}

    def at_y(d):
        return {"rows": ((y + d) % Y) * Z + z}

    def at_feat(d):
        return {"feat": (me + d) % FEAT}

    def at_x(d):
        return {"feat": ((x + d) % X) * 2 + core}

    def at_plane(dy, d):
        return {"rows": ((y + dy) % Y) * Z + z, "feat": (me + d) % FEAT}

    sibling = {"feat": x * 2 + 1 - core}

    loads = [pltpu.make_async_copy(a, b, lsem.at[3 + i]) for i, (a, b) in enumerate(
        ((codes_h, codes), (node_h, node), (boot_h, boot), (ph_h, ph)))]
    for c in loads:
        c.start()
    barrier = pltpu.get_barrier_semaphore()
    for d in range(1, FEAT):
        pl.semaphore_signal(barrier, inc=1, device_id=at_feat(d), device_id_type=MESH)
    for d in range(1, Z):
        pl.semaphore_signal(barrier, inc=1, device_id=at_z(d), device_id_type=MESH)
    for dy in range(1, Y):
        for d in range(FEAT):
            pl.semaphore_signal(barrier, inc=1, device_id=at_plane(dy, d), device_id_type=MESH)

    for c in loads:
        c.wait()
    cb[z, :, 0:RD] = codes[...].astype(F32).astype(BF16)
    for q in range(4):
        nq = node[pl.ds(q, FEAT, stride=4), :].astype(F32)
        wq = boot[pl.ds(q, FEAT, stride=4), :].astype(F32)
        both = jnp.concatenate([nq, wq], axis=0)
        cb[z, :, RD + 128 * q:RD + 128 * (q + 1)] = both.astype(BF16)

    pl.semaphore_wait(barrier, Z - 1 + Y * FEAT - 1)

    sends = []

    def send(what, src, dst, dev):
        i = len(sends)
        copy = pltpu.make_async_remote_copy(
            src_ref=src, dst_ref=dst, send_sem=ssem.at[i], recv_sem=rsem.at[i],
            device_id=dev, device_id_type=MESH)
        copy.start()
        sends.append(copy)
        return copy

    def row_block(i):
        return pl.ds(pl.multiple_of(i * CH, CH), CH)

    mine = pl.ds(pl.multiple_of(me * 128, 128), 128)

    def quarter(j):
        return pl.ds(pl.multiple_of(j * 128 + y * 32, 32), 32)

    own_q = om.at[pl.ds(pl.multiple_of(y * 32, 32), 32), :]
    om_in = [send("om", own_q, om_buf.at[quarter(me), :], at_x(d)) for d in (2, 1, 3)]
    om_sib = send("om", om, om_buf.at[mine, :], sibling)
    c_r = send("codes", cb.at[z], cb.at[z], at_z(1))
    c_l = send("codes", cb.at[z], cb.at[z], at_z(-1))
    t_in = []
    for d in (4, 5, 3, 2, 6, 1, 7):
        peer = (me + d) % FEAT
        t_in.append(send("t", tg.at[row_block(peer), :], t_buf.at[:, mine], at_feat(d)))
    own_t = pltpu.make_async_copy(tg.at[row_block(me), :], t_buf.at[:, mine], lsem.at[0])
    own_t.start()
    own_o = pltpu.make_async_copy(om, om_buf.at[mine, :], lsem.at[1])
    own_o.start()

    def one_hot(zs, start, which):
        c = cb[zs, :, pl.ds(start, CH)]
        w = jnp.broadcast_to(x32[pl.ds(which + FEAT, 1), :], (FD, CH)).astype(BF16)
        zero = jnp.zeros_like(w)
        return [jnp.where(c == jnp.asarray(b, BF16), w, zero) for b in range(BINS)]

    x32[...] = cb[z, :, RD:EXT].astype(F32)
    acc[...] = jnp.zeros_like(acc)
    oh[1] = jnp.zeros_like(oh[1])
    rn[1] = jnp.zeros_like(rn[1])
    nt = jnp.zeros((FD, BINS * FD), F32)
    acc_t = proj.at[0:FD, :]
    acc_t[...] = nt

    @pl.loop(0, FEAT)
    def _(jj):
        for b, part in enumerate(one_hot(z, pl.multiple_of(jj * CH, CH), jj)):
            oh[0, b * FD:(b + 1) * FD, :] = part
        nd = jnp.broadcast_to(x32[pl.ds(jj, 1), :], (FD, CH)).astype(BF16)
        ids = iota((FD, CH), 0).astype(F32).astype(BF16)
        noh = jnp.where(nd == ids, jnp.ones_like(nd), jnp.zeros_like(nd))
        acc_t[...] += lax.dot_general(noh, oh[0], NT, preferred_element_type=F32)

    tl = acc_t[0:NODES, :]
    r_id, l_id = iota((BINS * FD, 128), 0), iota((BINS * FD, 128), 1)
    for yy in range(Y):
        sel = (r_id // FD == l_id // 4) & (r_id % FD == 4 * yy + l_id % 4)
        ts[yy] = jnp.dot(tl, sel.astype(F32), precision=HIGH, preferred_element_type=F32)
    ty_in = [send("ty", ts.at[(y + d) % Y], ta.at[d], at_y(d)) for d in (2, 1, 3)]

    phc[...] = jnp.broadcast_to(ph[...], (128, R)).T

    c_r.wait_recv()
    c_l.wait_recv()
    c_r = send("codes", cb.at[(z + Z - 1) % Z], cb.at[(z + Z - 1) % Z], at_z(1))
    c_l = send("codes", cb.at[(z + 1) % Z], cb.at[(z + 1) % Z], at_z(-1))

    om_y = []
    for i, d in enumerate((2, 1, 3)):
        om_in[i].wait_recv()
    for d in (2, 1, 3):
        blk = om_buf.at[quarter(((x + d) % X) * 2 + core), :]
        for dy in (2, 1, 3):
            om_y.append(send("om", blk, blk, at_y(dy)))

    for c in ty_in:
        c.wait_recv()
    tsum[...] = ts[y] + ta[1] + ta[2] + ta[3]
    tz_in = [send("tz", tsum, tb.at[d], at_z(d)) for d in range(1, Z)]

    for c in om_y:
        c.wait_recv()
    om_fwd = [om_sib]
    for d in (1, 2, 3):
        src = pl.ds(pl.multiple_of((((x + d) % X) * 2 + core) * 128, 128), 128)
        om_fwd.append(send("omf", om_buf.at[src, :], om_buf.at[src, :], sibling))

    c_r.wait_recv()
    c_l.wait_recv()
    c_r = send("codes", cb.at[(z + Z - 2) % Z], cb.at[(z + Z - 2) % Z], at_z(1))
    c_l = send("codes", cb.at[(z + 2) % Z], cb.at[(z + 2) % Z], at_z(-1))

    own_o.wait()
    for c in om_fwd:
        c.wait_recv()
    omt[...] = om_buf[...].astype(F32).T.astype(BF16)

    own_t.wait()
    for c in t_in:
        c.wait_recv()
    proj[...] = lax.dot_general(omt[...], t_buf[...], NT, preferred_element_type=F32)
    scaling = math.sqrt(2.0 / R)

    @pl.loop(0, R // 32)
    def _(i):
        at = pl.ds(pl.multiple_of(i * 32, 32), 32)
        column = phc[at, :]
        for q in range(CH // 128):
            lane = slice(128 * q, 128 * (q + 1))
            ft[i, :, lane] = (scaling * cosine(proj[at, lane] + column)).astype(BF16)

    own_f = pltpu.make_async_copy(ft.at[z], fb.at[me, z], lsem.at[2])
    own_f.start()
    z_in = [None]
    for k in range(1, Z):
        z_in.append(send("fz", ft.at[(z - DELTA[k] + Z) % Z], fb.at[me, z], at_z(-DELTA[k])))
    own_f.wait()

    def product(h):
        return lax.dot_general(oh[h], rn[h], NT, preferred_element_type=F32)

    def hist(zs, first, last):
        x32[...] = cb[zs, :, RD:EXT].astype(F32)

        @pl.loop(first, last)
        def _(i):
            chip = (x + i + (i // 2) * (1 - 2 * (i % 2))) % X
            done = []
            for h in range(2):
                done.append(product(1 - h))
                jj = 2 * chip + h
                for b, part in enumerate(one_hot(zs, pl.multiple_of(jj * CH, CH), jj)):
                    oh[h, b * FD:(b + 1) * FD, :] = part
                nd = jnp.broadcast_to(x32[pl.ds(jj, 1), :], (FD, CH)).astype(BF16)
                f = fb[jj, zs]
                zero = jnp.zeros((FD, CH), BF16)
                for n in range(NODES):
                    mask = nd == jnp.asarray(n, BF16)
                    for g in range(CO // FD):
                        rn[h, n * CO + g * FD:n * CO + (g + 1) * FD, :] = jnp.where(
                            mask, f[g * FD:(g + 1) * FD], zero)
            acc[...] += done[0] + done[1]

    a_in, b_in, c_in = {}, {}, {}

    def from_x(d):
        return ((x + d) % X) * 2 + core

    def stage_a(k, zs):
        if k > 0:
            z_in[k].wait_recv()
        blk = fb.at[me, zs]
        a_in[k] = [send("fx", blk, blk, at_x(1)), send("fx", blk, blk, at_x(3)),
                   send("fs", blk, blk, sibling), send("fo", blk, blk, at_x(2))]

    def stage_b(k, zs):
        a_in[k][0].wait_recv()
        a_in[k][1].wait_recv()
        left, right = fb.at[from_x(3), zs], fb.at[from_x(1), zs]
        b_in[k] = [a_in[k][3], send("fs", left, left, sibling), send("fs", right, right, sibling)]

    def stage_c(k, zs):
        b_in[k][0].wait_recv()
        opp = fb.at[from_x(2), zs]
        c_in[k] = send("fs", opp, opp, sibling)

    def stage_s(k, zs):
        a_in[k][2].wait_recv()
        hist(zs, 0, 1)

    def stage_n(k, zs):
        b_in[k][1].wait_recv()
        b_in[k][2].wait_recv()
        hist(zs, 1, 3)

    def stage_o(k, zs):
        c_in[k].wait_recv()
        hist(zs, 3, 4)

    stages = {"A": stage_a, "B": stage_b, "C": stage_c, "S": stage_s, "N": stage_n, "O": stage_o}

    def run(*order):
        for item in order:
            k = int(item[1])
            stages[item[0]](k, (z + DELTA[k] + Z) % Z)

    run("A0", "S0", "A1", "A2", "B0")
    c_r.wait_recv()
    c_l.wait_recv()
    lo, hi = pl.ds(0, EXT // 2), pl.ds(EXT // 2, EXT // 2)
    c_r = send("codes", cb.at[(z + Z - 3) % Z, :, lo], cb.at[(z + Z - 3) % Z, :, lo], at_z(1))
    c_l = send("codes", cb.at[(z + 3) % Z, :, hi], cb.at[(z + 3) % Z, :, hi], at_z(-1))
    run("C0", "S1", "S2", "N0", "A3", "A4", "B1", "B2", "O0", "S3", "S4", "C1", "C2", "N1",
        "N2", "A5", "A6", "B3", "B4", "O1", "O2", "S5", "S6", "C3", "C4", "N3", "N4", "A7",
        "B5", "B6", "O3", "O4")
    c_r.wait_recv()
    c_l.wait_recv()
    run("S7", "C5", "C6", "N5", "N6", "B7", "C7", "O5", "O6", "N7", "O7")
    acc[...] += product(1)
    for yy in range(Y):
        half, sub = yy // 2, yy % 2
        for bp in range(BINS // 2):
            even = acc[(2 * bp) * FD + 8 * half:(2 * bp) * FD + 8 * half + 8, :]
            odd = acc[(2 * bp + 1) * FD + 8 * half:(2 * bp + 1) * FD + 8 * half + 8, :]
            low = iota((8, R), 0) < 4
            if sub == 0:
                sb[yy, 8 * bp:8 * bp + 8, :] = jnp.where(low, even, pltpu.roll(odd, 4, 0))
            else:
                sb[yy, 8 * bp:8 * bp + 8, :] = jnp.where(low, pltpu.roll(even, 4, 0), odd)
    y_in = [send("y", sb.at[(y + d) % Y], rb.at[d], at_y(d)) for d in (2, 1, 3)]

    for c in tz_in:
        c.wait_recv()
    total = tsum[...]
    for d in range(1, Z):
        total = total + tb[d]
    r128, l128 = iota((128, 128), 0), iota((128, 128), 1)
    same = r128 % 4 == l128 % 4
    upto = (same & (l128 // 4 <= r128 // 4)).astype(F32)
    every = same.astype(F32)
    left_n = lax.dot_general(total, upto, NT, precision=HIGH, preferred_element_type=F32)
    all_n = lax.dot_general(total, every, NT, precision=HIGH, preferred_element_type=F32)
    right_n = all_n - left_n
    factor = left_n * right_n / all_n
    expand = (iota((NODES, R), 1) // CO == iota((NODES, R), 0)).astype(F32)
    left_w = lax.dot_general(1.0 / jnp.maximum(left_n, 1.0), expand, TN,
                             precision=HIGH, preferred_element_type=F32)
    right_w = lax.dot_general(1.0 / jnp.maximum(right_n, 1.0), expand, TN,
                              precision=HIGH, preferred_element_type=F32)

    for c in y_in:
        c.wait_recv()
    summed = sb[y] + rb[1] + rb[2] + rb[3]
    left = jnp.dot(upto, summed, precision=HIGH, preferred_element_type=F32)
    whole = jnp.dot(every, summed, precision=HIGH, preferred_element_type=F32)
    differ = left * left_w - (whole - left) * right_w
    gb[z] = lax.dot_general(expand, differ * differ, NT, precision=HIGH,
                            preferred_element_type=F32)
    g_in = [send("g", gb.at[z], gb.at[z], at_z(d)) for d in (4, 3, 5, 2, 6, 1, 7)]
    for c in g_in:
        c.wait_recv()
    norm = gb[0]
    for d in range(1, Z):
        norm = norm + gb[d]
    gains = factor * norm

    top = jnp.max(jnp.where(iota((NODES, 128), 1) < 4 * (BINS - 1), gains, -jnp.inf),
                  axis=1, keepdims=True)
    diagonal = iota((NODES, 128), 1) == iota((NODES, 128), 0)
    bm[...] = jnp.max(jnp.where(diagonal, top, -jnp.inf), axis=0, keepdims=True)
    b_in = [send("best", bm, by.at[dy, d], at_plane(dy, d))
            for dy in (2, 1, 3, 0) for d in (4, 5, 3, 2, 6, 1, 7, 0) if dy + d]
    pick = (r128 == 4 * l128 + z // 2).astype(F32)
    picked = jnp.dot(gains, pick, precision=HIGH, preferred_element_type=F32)
    out[...] = jnp.where(z % 2 == 0, picked[0:4], picked[4:8])[:, 0:BINS - 1]
    for c in b_in:
        c.wait_recv()
    top = bm[...]
    for dy in range(Y):
        for d in range(FEAT):
            if dy + d:
                top = jnp.maximum(top, by[dy, d])
    best[...] = top
    for c in sends:
        c.wait_send()


N_SENDS = 160


def body(targets, omega, phase, codes, node, boot_counts):
    vmem = pl.BlockSpec(memory_space=pltpu.VMEM)
    gains, best = pl.pallas_call(
        kernel,
        out_shape=(jax.ShapeDtypeStruct((4, BINS - 1), F32),
                   jax.ShapeDtypeStruct((1, 128), F32)),
        in_specs=[pl.BlockSpec(memory_space=pltpu.MemorySpace.HBM)] * 6,
        out_specs=(vmem, vmem),
        scratch_shapes=[
            pltpu.VMEM((1, R), F32),
            pltpu.VMEM((FD, RD), jnp.int32),
            pltpu.VMEM((RD // 128, 128), jnp.int32),
            pltpu.VMEM((RD // 128, 128), jnp.int32),
            pltpu.VMEM((CH, 1024), BF16),
            pltpu.VMEM((1024, R), BF16),
            pltpu.VMEM((R, 1024), BF16),
            pltpu.VMEM((R, 128), F32),
            pltpu.VMEM((Z, FD, EXT), BF16),
            pltpu.VMEM((2 * FEAT, CH), F32),
            pltpu.VMEM((2, BINS * FD, CH), BF16),
            pltpu.VMEM((2, NODES * CO, CH), BF16),
            pltpu.VMEM((Z, CO, CH), BF16),
            pltpu.VMEM((R, CH), F32),
            pltpu.VMEM((FEAT, Z, CO, CH), BF16),
            pltpu.VMEM((BINS * FD, R), F32),
            pltpu.VMEM((Y, 128, R), F32),
            pltpu.VMEM((Y, 128, R), F32),
            pltpu.VMEM((Y, NODES, 128), F32),
            pltpu.VMEM((Y, NODES, 128), F32),
            pltpu.VMEM((NODES, 128), F32),
            pltpu.VMEM((Z, NODES, 128), F32),
            pltpu.VMEM((Z, NODES, 128), F32),
            pltpu.VMEM((1, 128), F32),
            pltpu.VMEM((Y, FEAT, 1, 128), F32),
            pltpu.SemaphoreType.DMA((N_SENDS,)),
            pltpu.SemaphoreType.DMA((N_SENDS,)),
            pltpu.SemaphoreType.DMA((7,)),
        ],
        compiler_params=pltpu.CompilerParams(
            collective_id=0, has_side_effects=True),
        name="forest_level",
    )(targets, omega, phase.reshape(1, R), codes.T,
      node.reshape(RD // 128, 128), boot_counts.reshape(RD // 128, 128))
    return gains, best[0, :NODES]


def solution(mesh):
    in_specs = (P("rows", "feat"), P("feat", None), P(), P("rows", "feat"), P("rows"), P("rows"))
    out_specs = (P(("feat", "rows"), None), P())
    return jax.shard_map(body, mesh=mesh, in_specs=in_specs, out_specs=out_specs, check_vma=False)
```

```python
import functools
import math

import jax
import jax.numpy as jnp
from jax import lax
from jax.experimental import pallas as pl
from jax.experimental.pallas import tpu as pltpu
from jax.sharding import PartitionSpec as P

MESH = pl.DeviceIdType.MESH
HIGH = lax.Precision.HIGHEST
F32 = jnp.float32
BF16 = jnp.bfloat16

R = 256
BINS = 32
NODES = 8
X = 4
Y = 4
Z = 8
FEAT = 2 * X
FD = 16
RD = 4096
CH = RD // FEAT
CO = R // Z
EXT = RD + CH
DELTA = (0, 1, -1, 2, -2, 3, -3, 4)

NT = (((1,), (1,)), ((), ()))
TN = (((0,), (0,)), ((), ()))

TWO_PI = 2.0 * math.pi
C1 = 6.28125
C2 = TWO_PI - C1
COS = [(-1.0) ** i / math.factorial(2 * i) for i in range(9)]


def cosine(v):
    turns = jnp.floor(v * (1.0 / TWO_PI) + 0.5)
    r = (v - turns * C1) - turns * C2
    x = r * r
    acc = jnp.full_like(x, COS[8])
    for c in COS[7::-1]:
        acc = acc * x + c
    return acc


def iota(shape, dim):
    return lax.broadcasted_iota(jnp.int32, shape, dim)


def kernel(tg, om, ph_h, codes_h, node_h, boot_h, out, best,
           ph, codes, node, boot, t_buf, om_buf, omt, phc, cb, x32, oh, rn, ft, proj, fb, acc, sb, s16, r16, xs, xr, mu, mr,
           ts, ta, tsum, tb, gb, bm, by, ssem, rsem, lsem):
    rows = lax.axis_index("rows")
    me = lax.axis_index("feat")
    y, z = rows // Z, rows % Z
    x, core = me // 2, me % 2

    def at_z(d):
        return {"rows": y * Z + (z + d + Z) % Z}

    def at_y(d):
        return {"rows": ((y + d) % Y) * Z + z}

    def at_feat(d):
        return {"feat": (me + d) % FEAT}

    def at_x(d):
        return {"feat": ((x + d) % X) * 2 + core}

    def at_plane(dy, d):
        return {"rows": ((y + dy) % Y) * Z + z, "feat": (me + d) % FEAT}

    sibling = {"feat": x * 2 + 1 - core}

    loads = [pltpu.make_async_copy(a, b, lsem.at[3 + i]) for i, (a, b) in enumerate(
        ((codes_h, codes), (node_h, node), (boot_h, boot), (ph_h, ph)))]
    for c in loads:
        c.start()
    barrier = pltpu.get_barrier_semaphore()
    for d in range(1, FEAT):
        pl.semaphore_signal(barrier, inc=1, device_id=at_feat(d), device_id_type=MESH)
    for d in range(1, Z):
        pl.semaphore_signal(barrier, inc=1, device_id=at_z(d), device_id_type=MESH)
    for dy in range(1, Y):
        for d in range(FEAT):
            pl.semaphore_signal(barrier, inc=1, device_id=at_plane(dy, d), device_id_type=MESH)

    for c in loads:
        c.wait()
    cb[z, :, 0:RD] = codes[...].astype(F32).astype(BF16)
    for q in range(4):
        nq = node[pl.ds(q, FEAT, stride=4), :].astype(F32)
        wq = boot[pl.ds(q, FEAT, stride=4), :].astype(F32)
        both = jnp.concatenate([nq, wq], axis=0)
        cb[z, :, RD + 128 * q:RD + 128 * (q + 1)] = both.astype(BF16)

    pl.semaphore_wait(barrier, Z - 1 + Y * FEAT - 1)

    sends = []

    def send(what, src, dst, dev):
        i = len(sends)
        copy = pltpu.make_async_remote_copy(
            src_ref=src, dst_ref=dst, send_sem=ssem.at[i], recv_sem=rsem.at[i],
            device_id=dev, device_id_type=MESH)
        copy.start()
        sends.append(copy)
        return copy

    def row_block(i):
        return pl.ds(pl.multiple_of(i * CH, CH), CH)

    mine = pl.ds(pl.multiple_of(me * 128, 128), 128)

    def quarter(j):
        return pl.ds(pl.multiple_of(j * 128 + y * 32, 32), 32)

    own_q = om.at[pl.ds(pl.multiple_of(y * 32, 32), 32), :]
    om_in = [send("om", own_q, om_buf.at[quarter(me), :], at_x(d)) for d in (2, 1, 3)]
    om_sib = send("om", om, om_buf.at[mine, :], sibling)
    c_r = send("codes", cb.at[z], cb.at[z], at_z(1))
    c_l = send("codes", cb.at[z], cb.at[z], at_z(-1))
    t_in = []
    for d in (4, 5, 3, 2, 6, 1, 7):
        peer = (me + d) % FEAT
        t_in.append(send("t", tg.at[row_block(peer), :], t_buf.at[:, mine], at_feat(d)))
    own_t = pltpu.make_async_copy(tg.at[row_block(me), :], t_buf.at[:, mine], lsem.at[0])
    own_t.start()
    own_o = pltpu.make_async_copy(om, om_buf.at[mine, :], lsem.at[1])
    own_o.start()

    def one_hot(zs, start, which):
        c = cb[zs, :, pl.ds(start, CH)]
        w = jnp.broadcast_to(x32[pl.ds(which + FEAT, 1), :], (FD, CH)).astype(BF16)
        zero = jnp.zeros_like(w)
        return [jnp.where(c == jnp.asarray(b, BF16), w, zero) for b in range(BINS)]

    x32[...] = cb[z, :, RD:EXT].astype(F32)
    acc[...] = jnp.zeros_like(acc)
    oh[1] = jnp.zeros_like(oh[1])
    rn[1] = jnp.zeros_like(rn[1])
    nt = jnp.zeros((FD, BINS * FD), F32)
    acc_t = proj.at[0:FD, :]
    acc_t[...] = nt

    @pl.loop(0, FEAT)
    def _(jj):
        for b, part in enumerate(one_hot(z, pl.multiple_of(jj * CH, CH), jj)):
            oh[0, b * FD:(b + 1) * FD, :] = part
        nd = jnp.broadcast_to(x32[pl.ds(jj, 1), :], (FD, CH)).astype(BF16)
        ids = iota((FD, CH), 0).astype(F32).astype(BF16)
        noh = jnp.where(nd == ids, jnp.ones_like(nd), jnp.zeros_like(nd))
        acc_t[...] += lax.dot_general(noh, oh[0], NT, preferred_element_type=F32)

    tl = acc_t[0:NODES, :]
    r_id, l_id = iota((BINS * FD, 128), 0), iota((BINS * FD, 128), 1)
    for yy in range(Y):
        sel = (r_id // FD == l_id // 4) & (r_id % FD == 4 * yy + l_id % 4)
        ts[yy] = jnp.dot(tl, sel.astype(F32), precision=HIGH, preferred_element_type=F32)
    tz_in = [send("tz", ts, tb.at[d], at_z(d)) for d in range(1, Z)]

    phc[...] = jnp.broadcast_to(ph[...], (128, R)).T

    c_r.wait_recv()
    c_l.wait_recv()
    c_r = send("codes", cb.at[(z + Z - 1) % Z], cb.at[(z + Z - 1) % Z], at_z(1))
    c_l = send("codes", cb.at[(z + 1) % Z], cb.at[(z + 1) % Z], at_z(-1))

    om_y = []
    for i, d in enumerate((2, 1, 3)):
        om_in[i].wait_recv()
    for d in (2, 1, 3):
        blk = om_buf.at[quarter(((x + d) % X) * 2 + core), :]
        for dy in (2, 1, 3):
            om_y.append(send("om", blk, blk, at_y(dy)))

    for c in tz_in:
        c.wait_recv()
    line = ts[...]
    for d in range(1, Z):
        line = line + tb[d]
    tsum[...] = line
    ty_in = [send("ty", tsum.at[(y + d) % Y], ta.at[d], at_y(d)) for d in (2, 1, 3)]

    for c in om_y:
        c.wait_recv()
    om_fwd = [om_sib]
    for d in (1, 2, 3):
        src = pl.ds(pl.multiple_of((((x + d) % X) * 2 + core) * 128, 128), 128)
        om_fwd.append(send("omf", om_buf.at[src, :], om_buf.at[src, :], sibling))

    c_r.wait_recv()
    c_l.wait_recv()
    c_r = send("codes", cb.at[(z + Z - 2) % Z], cb.at[(z + Z - 2) % Z], at_z(1))
    c_l = send("codes", cb.at[(z + 2) % Z], cb.at[(z + 2) % Z], at_z(-1))

    own_o.wait()
    for c in om_fwd:
        c.wait_recv()
    omt[...] = om_buf[...].astype(F32).T.astype(BF16)

    expand = (iota((NODES, R), 1) // CO == iota((NODES, R), 0)).astype(F32)

    def spread(counts):
        return lax.dot_general(counts, expand, TN, precision=HIGH, preferred_element_type=F32)

    for c in ty_in:
        c.wait_recv()
    for yy in range(Y):
        xs[yy] = spread(tsum[yy])
    for d in range(1, Y):
        xr[d] = spread(ta[d])

    own_t.wait()
    for c in t_in:
        c.wait_recv()
    proj[...] = lax.dot_general(omt[...], t_buf[...], NT, preferred_element_type=F32)
    scaling = math.sqrt(2.0 / R)

    @pl.loop(0, R // 32)
    def _(i):
        at = pl.ds(pl.multiple_of(i * 32, 32), 32)
        column = phc[at, :]
        for q in range(CH // 128):
            lane = slice(128 * q, 128 * (q + 1))
            ft[i, :, lane] = (scaling * cosine(proj[at, lane] + column)).astype(BF16)

    own_f = pltpu.make_async_copy(ft.at[z], fb.at[me, z], lsem.at[2])
    own_f.start()
    z_in = [None]
    for k in range(1, Z):
        z_in.append(send("fz", ft.at[(z - DELTA[k] + Z) % Z], fb.at[me, z], at_z(-DELTA[k])))
    own_f.wait()

    def product(h):
        return lax.dot_general(oh[h], rn[h], NT, preferred_element_type=F32)

    def hist(zs, first, last):
        x32[...] = cb[zs, :, RD:EXT].astype(F32)

        @pl.loop(first, last)
        def _(i):
            chip = (x + i + (i // 2) * (1 - 2 * (i % 2))) % X
            done = []
            for h in range(2):
                done.append(product(1 - h))
                jj = 2 * chip + h
                for b, part in enumerate(one_hot(zs, pl.multiple_of(jj * CH, CH), jj)):
                    oh[h, b * FD:(b + 1) * FD, :] = part
                nd = jnp.broadcast_to(x32[pl.ds(jj, 1), :], (FD, CH)).astype(BF16)
                f = fb[jj, zs]
                zero = jnp.zeros((FD, CH), BF16)
                for n in range(NODES):
                    mask = nd == jnp.asarray(n, BF16)
                    for g in range(CO // FD):
                        rn[h, n * CO + g * FD:n * CO + (g + 1) * FD, :] = jnp.where(
                            mask, f[g * FD:(g + 1) * FD], zero)
            acc[...] += done[0] + done[1]

    a_in, b_in, c_in = {}, {}, {}

    def from_x(d):
        return ((x + d) % X) * 2 + core

    def stage_a(k, zs):
        if k > 0:
            z_in[k].wait_recv()
        blk = fb.at[me, zs]
        a_in[k] = [send("fx", blk, blk, at_x(1)), send("fx", blk, blk, at_x(3)),
                   send("fs", blk, blk, sibling), send("fo", blk, blk, at_x(2))]

    def stage_b(k, zs):
        a_in[k][0].wait_recv()
        a_in[k][1].wait_recv()
        left, right = fb.at[from_x(3), zs], fb.at[from_x(1), zs]
        b_in[k] = [a_in[k][3], send("fs", left, left, sibling), send("fs", right, right, sibling)]

    def stage_c(k, zs):
        b_in[k][0].wait_recv()
        opp = fb.at[from_x(2), zs]
        c_in[k] = send("fs", opp, opp, sibling)

    def stage_s(k, zs):
        a_in[k][2].wait_recv()
        hist(zs, 0, 1)

    def stage_n(k, zs):
        b_in[k][1].wait_recv()
        b_in[k][2].wait_recv()
        hist(zs, 1, 3)

    def stage_o(k, zs):
        c_in[k].wait_recv()
        hist(zs, 3, 4)

    stages = {"A": stage_a, "B": stage_b, "C": stage_c, "S": stage_s, "N": stage_n, "O": stage_o}

    def run(*order):
        for item in order:
            k = int(item[1])
            stages[item[0]](k, (z + DELTA[k] + Z) % Z)

    run("A0", "S0", "A1", "A2", "B0")
    c_r.wait_recv()
    c_l.wait_recv()
    lo, hi = pl.ds(0, EXT // 2), pl.ds(EXT // 2, EXT // 2)
    c_r = send("codes", cb.at[(z + Z - 3) % Z, :, lo], cb.at[(z + Z - 3) % Z, :, lo], at_z(1))
    c_l = send("codes", cb.at[(z + 3) % Z, :, hi], cb.at[(z + 3) % Z, :, hi], at_z(-1))
    run("C0", "S1", "S2", "N0", "A3", "A4", "B1", "B2", "O0", "S3", "S4", "C1", "C2", "N1",
        "N2", "A5", "A6", "B3", "B4", "O1", "O2", "S5", "S6", "C3", "C4", "N3", "N4", "A7",
        "B5", "B6", "O3", "O4")
    c_r.wait_recv()
    c_l.wait_recv()
    run("S7", "C5", "C6", "N5", "N6", "B7", "C7", "O5", "O6", "N7", "O7")
    acc[...] += product(1)
    weight = jnp.sum(jnp.sum(tsum[...], axis=0), axis=1, keepdims=True)
    mean = (jnp.sum(acc[...], axis=0, keepdims=True)
            / jnp.sum(expand * weight, axis=0, keepdims=True))
    mu[...] = mean
    y_in = [send("y", mu, mr.at[d], at_y(d)) for d in (2, 1, 3)]
    for yy in range(Y):
        half, sub = yy // 2, yy % 2
        for bp in range(BINS // 2):
            even = acc[(2 * bp) * FD + 8 * half:(2 * bp) * FD + 8 * half + 8, :]
            odd = acc[(2 * bp + 1) * FD + 8 * half:(2 * bp + 1) * FD + 8 * half + 8, :]
            low = iota((8, R), 0) < 4
            if sub == 0:
                sb[yy, 8 * bp:8 * bp + 8, :] = jnp.where(low, even, pltpu.roll(odd, 4, 0))
            else:
                sb[yy, 8 * bp:8 * bp + 8, :] = jnp.where(low, pltpu.roll(even, 4, 0), odd)
        s16[yy] = (sb[yy] - xs[yy] * mean).astype(BF16)
    y_in += [send("y", s16.at[(y + d) % Y], r16.at[d], at_y(d)) for d in (2, 1, 3)]

    total = tsum[y] + ta[1] + ta[2] + ta[3]
    r128, l128 = iota((128, 128), 0), iota((128, 128), 1)
    same = r128 % 4 == l128 % 4
    upto = (same & (l128 // 4 <= r128 // 4)).astype(F32)
    every = same.astype(F32)
    left_n = lax.dot_general(total, upto, NT, precision=HIGH, preferred_element_type=F32)
    all_n = lax.dot_general(total, every, NT, precision=HIGH, preferred_element_type=F32)
    right_n = all_n - left_n
    factor = left_n * right_n / all_n
    left_w = lax.dot_general(1.0 / jnp.maximum(left_n, 1.0), expand, TN,
                             precision=HIGH, preferred_element_type=F32)
    right_w = lax.dot_general(1.0 / jnp.maximum(right_n, 1.0), expand, TN,
                              precision=HIGH, preferred_element_type=F32)

    for c in y_in:
        c.wait_recv()
    summed = sb[y]
    for d in range(1, Y):
        summed = summed + (r16[d].astype(F32) + xr[d] * mr[d])
    left = jnp.dot(upto, summed, precision=HIGH, preferred_element_type=F32)
    whole = jnp.dot(every, summed, precision=HIGH, preferred_element_type=F32)
    differ = left * left_w - (whole - left) * right_w
    gb[z] = lax.dot_general(expand, differ * differ, NT, precision=HIGH,
                            preferred_element_type=F32)
    g_in = [send("g", gb.at[z], gb.at[z], at_z(d)) for d in (4, 3, 5, 2, 6, 1, 7)]
    for c in g_in:
        c.wait_recv()
    norm = gb[0]
    for d in range(1, Z):
        norm = norm + gb[d]
    gains = factor * norm

    top = jnp.max(jnp.where(iota((NODES, 128), 1) < 4 * (BINS - 1), gains, -jnp.inf),
                  axis=1, keepdims=True)
    diagonal = iota((NODES, 128), 1) == iota((NODES, 128), 0)
    bm[...] = jnp.max(jnp.where(diagonal, top, -jnp.inf), axis=0, keepdims=True)
    b_in = [send("best", bm, by.at[dy, d], at_plane(dy, d))
            for dy in (2, 1, 3, 0) for d in (4, 5, 3, 2, 6, 1, 7, 0) if dy + d]
    pick = (r128 == 4 * l128 + z // 2).astype(F32)
    picked = jnp.dot(gains, pick, precision=HIGH, preferred_element_type=F32)
    out[...] = jnp.where(z % 2 == 0, picked[0:4], picked[4:8])[:, 0:BINS - 1]
    for c in b_in:
        c.wait_recv()
    top = bm[...]
    for dy in range(Y):
        for d in range(FEAT):
            if dy + d:
                top = jnp.maximum(top, by[dy, d])
    best[...] = top
    for c in sends:
        c.wait_send()


N_SENDS = 160


def body(targets, omega, phase, codes, node, boot_counts):
    vmem = pl.BlockSpec(memory_space=pltpu.VMEM)
    gains, best = pl.pallas_call(
        kernel,
        out_shape=(jax.ShapeDtypeStruct((4, BINS - 1), F32),
                   jax.ShapeDtypeStruct((1, 128), F32)),
        in_specs=[pl.BlockSpec(memory_space=pltpu.MemorySpace.HBM)] * 6,
        out_specs=(vmem, vmem),
        scratch_shapes=[
            pltpu.VMEM((1, R), F32),
            pltpu.VMEM((FD, RD), jnp.int32),
            pltpu.VMEM((RD // 128, 128), jnp.int32),
            pltpu.VMEM((RD // 128, 128), jnp.int32),
            pltpu.VMEM((CH, 1024), BF16),
            pltpu.VMEM((1024, R), BF16),
            pltpu.VMEM((R, 1024), BF16),
            pltpu.VMEM((R, 128), F32),
            pltpu.VMEM((Z, FD, EXT), BF16),
            pltpu.VMEM((2 * FEAT, CH), F32),
            pltpu.VMEM((2, BINS * FD, CH), BF16),
            pltpu.VMEM((2, NODES * CO, CH), BF16),
            pltpu.VMEM((Z, CO, CH), BF16),
            pltpu.VMEM((R, CH), F32),
            pltpu.VMEM((FEAT, Z, CO, CH), BF16),
            pltpu.VMEM((BINS * FD, R), F32),
            pltpu.VMEM((Y, 128, R), F32),
            pltpu.VMEM((Y, 128, R), BF16),
            pltpu.VMEM((Y, 128, R), BF16),
            pltpu.VMEM((Y, 128, R), F32),
            pltpu.VMEM((Y, 128, R), F32),
            pltpu.VMEM((1, R), F32),
            pltpu.VMEM((Y, 1, R), F32),
            pltpu.VMEM((Y, NODES, 128), F32),
            pltpu.VMEM((Y, NODES, 128), F32),
            pltpu.VMEM((Y, NODES, 128), F32),
            pltpu.VMEM((Z, Y, NODES, 128), F32),
            pltpu.VMEM((Z, NODES, 128), F32),
            pltpu.VMEM((1, 128), F32),
            pltpu.VMEM((Y, FEAT, 1, 128), F32),
            pltpu.SemaphoreType.DMA((N_SENDS,)),
            pltpu.SemaphoreType.DMA((N_SENDS,)),
            pltpu.SemaphoreType.DMA((7,)),
        ],
        compiler_params=pltpu.CompilerParams(
            collective_id=0, has_side_effects=True),
        name="forest_level",
    )(targets, omega, phase.reshape(1, R), codes.T,
      node.reshape(RD // 128, 128), boot_counts.reshape(RD // 128, 128))
    return gains, best[0, :NODES]


def solution(mesh):
    in_specs = (P("rows", "feat"), P("feat", None), P(), P("rows", "feat"), P("rows"), P("rows"))
    out_specs = (P(("feat", "rows"), None), P())
    return jax.shard_map(body, mesh=mesh, in_specs=in_specs, out_specs=out_specs, check_vma=False)
```
